128 devices in a mesh: row: 8 (over x, core), col: 16 (over y, z).
Axes of the slice: x: 4, y: 4, z: 4, core: 2. Of those that a mesh axis runs over, the one named last changes fastest.
Arguments:
- hamiltonian: float32 [16384, 2048], P('row', 'col'), may hold values from -0.09375 to 0.09375
- pattern: int32 [512, 64], P('row', 'col'), may hold values 0 or 1
- onsite: float32 [16384], P('row'), may hold values from -1 to 1
- members: int32 [128, 32], replicated, may hold values from 0 to 63, as said below
- orders: int32 [128], replicated, may hold values from 16 to 32, as said below
- intersection_inv: bfloat16 [16384, 3, 2048], P(('row', 'col')), may hold values from -6 to 6
Outputs:
- density: float32 [16384, 3, 2048], P(('row', 'col'))
The draws below stay inside these ranges and needn't reach their ends.
Inputs may be any that keep to these rules, and one draw needn't show every extreme that they name: `members`: each row holds 32 distinct team block indices; the first 4 of row g are (g mod 16) * 4 onward in rising order. `orders`: some group has all 32 members active.
All inputs are finite; a program needn't handle non-finite values. No bound on the sum of `pattern` on one device may be relied on, other than what follows from the above.
Results may differ from the reference program's by a relative error of at most 0.0027.
Values may be sent and summed in bfloat16 or wider, within the bound.
A program may use at most 256 MiB of HBM per device.

```python
import jax
import jax.numpy as jnp
from jax import lax

BLOCK = 32
OWN_BLOCKS = 4
MEMBERS = 32
TEAMS = 8
SLOTS = 16
TEAM_BLOCKS = 64
TEAM_WIDTH = 2048
GROUPS = 128
ALL_ROWS = 16384


def draw_members(key, part):

    def one_group(group_index):
        slot_index = group_index % SLOTS
        own_blocks = slot_index * OWN_BLOCKS + jnp.arange(OWN_BLOCKS, dtype=jnp.int32)
        shuffled = jax.random.permutation(jax.random.fold_in(key, group_index), TEAM_BLOCKS).astype(jnp.int32)
        owned_flag = (shuffled >= slot_index * OWN_BLOCKS) & (shuffled < slot_index * OWN_BLOCKS + OWN_BLOCKS)
        ranking = owned_flag.astype(jnp.int32) * TEAM_BLOCKS + jnp.arange(TEAM_BLOCKS, dtype=jnp.int32)
        picked = shuffled[jnp.argsort(ranking, stable=True)]
        return jnp.concatenate([own_blocks, picked[:MEMBERS - OWN_BLOCKS]]).astype(jnp.int32)
    return jax.vmap(one_group)(jnp.arange(GROUPS, dtype=jnp.int32))


def draw_orders(key, part):
    counts = jax.random.randint(key, (GROUPS,), MEMBERS // 2, MEMBERS + 1)
    fullest = jax.random.randint(jax.random.fold_in(key, 7), (), 0, GROUPS)
    return jnp.where(jnp.arange(GROUPS) == fullest, MEMBERS, counts).astype(jnp.int32)


def touch_ends(entries, rng, least, high):
    extent = entries.shape
    index_at = [jax.random.randint(jax.random.fold_in(rng, axis), (), 0, extent[axis]) for axis in range(len(extent))]
    entries = entries.at[tuple(index_at)].set(least)
    longest = extent.index(max(extent))
    index_at[longest] = (index_at[longest] + 1) % extent[longest]
    return entries.at[tuple(index_at)].set(high)


def level_of(key, shape, pieces, low, largest):
    level, own = 1.0, jax.random.fold_in(key, 6)
    for dim, parts in pieces:
        heights = jnp.exp(jax.random.uniform(jax.random.fold_in(own, dim), (parts,), jnp.float32, low / len(pieces), largest / len(pieces)))
        level = level * jnp.repeat(heights, shape[dim] // parts).reshape([-1 if axis == dim else 1 for axis in range(len(shape))])
    return level


def noise(key, extent, deviation, reach, shards=(), kind=jnp.bfloat16):
    gain = level_of(key, extent, shards, -0.22, 0.18) if shards else 1.0
    values = jax.random.normal(key, extent, jnp.float32) * deviation * gain
    return jnp.minimum(jnp.maximum(values, -reach), reach).astype(kind)


def setup_inputs(seed: int = 0) -> dict:
    key_of = jax.random.split(jax.random.key(seed), 7)
    return {
        "hamiltonian": noise(key_of[0], (ALL_ROWS, TEAM_WIDTH), (4 * MEMBERS * BLOCK) ** -0.5, 0.09375, ((0, 8), (1, 16)), jnp.float32),
        "pattern": touch_ends((jax.random.randint(key_of[1], (TEAMS * TEAM_BLOCKS, TEAM_BLOCKS), 0, 4) < 3).astype(jnp.int32), jax.random.fold_in(key_of[1], 1), 0, 1),
        "onsite": jnp.clip(jax.random.uniform(key_of[2], (ALL_ROWS,), jnp.float32, -1.0, 1.0) * level_of(key_of[2], (ALL_ROWS,), ((0, 8),), -0.4, 0.0), -1.0, 1.0),
        "members": draw_members(jax.random.fold_in(key_of[6], 71), 0),
        "orders": draw_orders(jax.random.fold_in(key_of[6], 71), 0),
        "intersection_inv": noise(key_of[5], (ALL_ROWS, 3, TEAM_WIDTH), 0.7, 6.0, ((0, 128),)),
    }


def element_rows(blocks):
    offsets = jnp.arange(BLOCK, dtype=jnp.int32)
    return (blocks[..., :, None] * BLOCK + offsets).reshape(blocks.shape[:-1] + (-1,)).astype(jnp.int32)

def sign_columns(submatrix, active_count, own_width):
    squares = jnp.sum(submatrix * submatrix)
    factor = jnp.sqrt(active_count.astype(jnp.float32) * BLOCK / (4.0 * (squares + 1e-06)))
    initial = factor * submatrix
    square = jnp.dot(initial, initial, precision=lax.Precision.HIGHEST, preferred_element_type=jnp.float32)
    first_step = 0.5 * (3.0 * initial - jnp.dot(initial, square, precision=lax.Precision.HIGHEST, preferred_element_type=jnp.float32))
    left_cols = first_step[:, :own_width]
    inner_prod = jnp.dot(first_step, left_cols, precision=lax.Precision.HIGHEST, preferred_element_type=jnp.float32)
    return 0.5 * (3.0 * left_cols - jnp.dot(first_step, inner_prod, precision=lax.Precision.HIGHEST, preferred_element_type=jnp.float32))

def reference(hamiltonian, pattern, onsite, members, orders, intersection_inv):
    own_width = OWN_BLOCKS * BLOCK
    weights = jnp.repeat(jnp.repeat(pattern.astype(jnp.float32), BLOCK, axis=0), BLOCK, axis=1)
    team_ham = (hamiltonian * weights).reshape(TEAMS, TEAM_WIDTH, TEAM_WIDTH)
    team_onsite = onsite.reshape(TEAMS, TEAM_WIDTH)

    def one_group(group_index):
        team_index = group_index // SLOTS
        row_ids = element_rows(members[group_index])
        block_ham = lax.dynamic_index_in_dim(team_ham, team_index, 0, keepdims=False)
        coupling = jnp.take(jnp.take(block_ham, row_ids, axis=0), row_ids, axis=1)
        active = jnp.repeat((jnp.arange(MEMBERS) < orders[group_index]).astype(jnp.float32), BLOCK)
        coupling = coupling * active[:, None] * active[None, :]
        diag_vals = jnp.take(lax.dynamic_index_in_dim(team_onsite, team_index, 0, keepdims=False), row_ids) * active
        submatrix = 0.5 * (coupling + coupling.T) + jnp.diag(diag_vals)
        return sign_columns(submatrix, orders[group_index], own_width).astype(jnp.bfloat16)
    sign_blocks = lax.map(one_group, jnp.arange(GROUPS, dtype=jnp.int32))
    rows_all = element_rows(members)
    team_of = jnp.arange(GROUPS, dtype=jnp.int32) // SLOTS
    slot_of = jnp.arange(GROUPS, dtype=jnp.int32) % SLOTS
    team_sign = jnp.zeros((TEAMS, TEAM_WIDTH, SLOTS, own_width), jnp.bfloat16)
    team_sign = team_sign.at[team_of[:, None], rows_all, slot_of[:, None]].set(sign_blocks)
    team_sign = team_sign.reshape(TEAMS, TEAM_WIDTH, TEAM_WIDTH)
    z_teams = intersection_inv.reshape(TEAMS, TEAM_WIDTH, 3, TEAM_WIDTH)

    def one_team(team_index):
        z_team = lax.dynamic_index_in_dim(z_teams, team_index, 0, keepdims=False)
        results = []
        for side_index in range(3):
            other_team = (team_index + side_index - 1) % TEAMS
            sign_team = lax.dynamic_index_in_dim(team_sign, other_team, 0, keepdims=False)
            results.append(jnp.dot(z_team[:, side_index, :], sign_team, preferred_element_type=jnp.float32))
        return jnp.stack(results, axis=1)
    density = lax.map(one_team, jnp.arange(TEAMS, dtype=jnp.int32))
    return density.reshape(ALL_ROWS, 3, TEAM_WIDTH)
```

```python
import jax
import jax.numpy as jnp
from jax import lax
from jax.experimental import pallas as pl
from jax.experimental.pallas import tpu as pltpu
from jax.sharding import PartitionSpec as P

BLOCK = 32
OWN_BLOCKS = 4
MEMBERS = 32
SLOTS = 16
TEAMS = 8
TEAM_BLOCKS = 64
TEAM_WIDTH = 2048
SUB = MEMBERS * BLOCK
OWN = OWN_BLOCKS * BLOCK
TILES = SUB // OWN
F32 = jnp.float32
BF16 = jnp.bfloat16
MESH = pl.DeviceIdType.MESH
SHARED = 12
LEAD = 10
RING_K = ((0, 3), (0, 1), (3, 2), (1, 2))


class Gather:
    def __init__(self, region, rows, send_sems, recv_sems, device):
        self.region, self.rows, self.device = region, rows, device
        self.send_sems, self.recv_sems = send_sems, recv_sems
        self.got = {(0, 0): {0, 1}}

    def copy(self, half, ring, k):
        source, landing = RING_K[k]
        step = 1 if k in (0, 2) else -1
        rows = self.rows // 2
        start, size = half * rows, rows
        if k >= 2:
            size = rows // 2
            start += size * (k - 2)

        def spot(offset):
            a, b = (offset, 0) if ring == 0 else (ring - 1, offset)
            return (b, a) if half == 0 else (a, b)

        along_z = (half == 0) == (ring == 0)
        n = half * 20 + ring * 4 + k
        return pltpu.make_async_remote_copy(
            src_ref=self.region(*spot(source), start, size),
            dst_ref=self.region(*spot(landing), start, size),
            send_sem=self.send_sems.at[n],
            recv_sem=self.recv_sems.at[n],
            device_id=self.device(0, step) if along_z else self.device(step, 0),
            device_id_type=MESH,
        ), spot(landing)

    def begin(self):
        for ring in (0, 1):
            for half in (0, 1):
                for k in (0, 1):
                    self.copy(half, ring, k)[0].start()

    def steps(self):
        order = [(0, 0), (0, 1), (1, 0), (1, 1), (0, 2), (0, 3), (4, 0), (4, 1), (2, 0), (2, 1), (1, 2), (1, 3)]
        order += [(3, 0), (3, 1), (4, 2), (4, 3), (2, 2), (2, 3), (3, 2), (3, 3)]
        seen = {}
        for ring, k in order:
            for half in (0, 1):
                copy, spot = self.copy(half, ring, k)
                copy.wait_recv()
                if k < 2:
                    self.copy(half, ring, k + 2)[0].start()
                whole = k < 2 or (half, ring, 5 - k) in seen
                seen[half, ring, k] = True
                done = None
                if ring == 0 and whole:
                    for j in (0, 1):
                        self.copy(half, RING_K[k][1] + 1, j)[0].start()
                if whole:
                    halves = self.got.setdefault(spot, set())
                    halves.add(half)
                    done = spot if len(halves) == 2 else None
                yield done

    def finish(self):
        for half in (0, 1):
            for ring in range(5):
                for k in range(4):
                    self.copy(half, ring, k)[0].wait_send()


def places():
    row, col = lax.axis_index("row"), lax.axis_index("col")
    y, z = col // 4, col % 4

    def device(dy, dz):
        return (row, ((y + dy + 4) % 4) * 4 + (z + dz + 4) % 4)

    return row, col, y, z, device


def greet(devices):
    barrier = pltpu.get_barrier_semaphore()
    for device in devices:
        pl.semaphore_signal(barrier, inc=1, device_id=device, device_id_type=MESH)
    pl.semaphore_wait(barrier, len(devices))


def sign_kernel(
    table, active, ham, pattern, onsite, out, own, onsites, left, rolled, turned, mat, diag, send_sems, recv_sems, *bufs
):
    row, col, y, z, device = places()
    near = [device(1, 0), device(3, 0), device(0, 1), device(0, 3)]
    lanes = lax.broadcasted_iota(jnp.int32, (OWN_BLOCKS, OWN), 1) // BLOCK
    spread = (lanes == lax.broadcasted_iota(jnp.int32, (OWN_BLOCKS, OWN), 0)).astype(F32)
    weights = lax.dot_general(
        pattern[...].astype(F32), spread, (((0,), (0,)), ((), ())), preferred_element_type=F32
    )
    for a in range(TEAM_BLOCKS):
        masked = ham[a * BLOCK : (a + 1) * BLOCK, :] * weights[a : a + 1, :]
        own[a] = masked
        bufs[0][a] = masked.astype(BF16)
    greet(near)
    gather = Gather(
        lambda oy, oz, start, size: bufs[oy * 4 + oz].at[pl.ds(start, size)], TEAM_BLOCKS, send_sems, recv_sems, device
    )
    gather.begin()
    for s in range(4):
        onsites[s * SLOTS : (s + 1) * SLOTS] = pltpu.roll(onsite[...], s * BLOCK, axis=1).reshape(SLOTS, 1, OWN)
    one_row = lax.broadcasted_iota(jnp.int32, (1, OWN), 1) // BLOCK

    def blocks(read, tile):
        pieces = [read(table[0, tile * 4 + q]).astype(F32) * active[0, tile * 4 + q] for q in range(4)]
        return jnp.concatenate(pieces, axis=0)

    @pl.loop(0, TILES)
    def _(tile):
        at = pl.ds(pl.multiple_of(tile * OWN, OWN), OWN)
        left[:, at] = blocks(lambda m: own[m], tile).T
        picked = jnp.zeros((1, OWN), F32)
        for q in range(4):
            line = onsites[table[3, tile * 4 + q]] * active[0, tile * 4 + q]
            picked = jnp.where(one_row == q, line, picked)
        diag[:, at] = picked

    def take_in(oy, oz):
        slot = oy * 4 + oz

        @pl.loop(0, TILES)
        def _(tile):
            x = blocks(lambda m: bufs[slot][m], tile)
            turned[slot, tile] = x.T.astype(BF16).reshape(4, BLOCK, OWN)
            rolled[slot * 4, tile] = x.astype(BF16)
            for s in (1, 2, 3):
                rolled[slot * 4 + s, tile] = pltpu.roll(x, s * BLOCK, axis=1).astype(BF16)

    take_in(0, 0)
    for spot in gather.steps():
        if spot:
            take_in(*spot)
    gather.finish()

    which = lax.broadcasted_iota(jnp.int32, (OWN, OWN), 1) // BLOCK
    eye = lax.broadcasted_iota(jnp.int32, (OWN, OWN), 0) == lax.broadcasted_iota(jnp.int32, (OWN, OWN), 1)

    def direct(up, across):
        tile = None
        for q in range(4):
            piece = rolled[table[1, across * 4 + q], up].astype(F32) * active[0, across * 4 + q]
            tile = piece if tile is None else jnp.where(which == q, piece, tile)
        return tile

    def mirrored(up, across):
        pieces = []
        for q in range(4):
            a = up * 4 + q
            pieces.append(turned[table[2, a], across, table[4, a]].astype(F32) * active[0, a])
        return jnp.concatenate(pieces, axis=0)

    def assemble(n, total):
        up, across = n // TILES, n % TILES
        tile = 0.5 * (direct(up, across) + mirrored(up, across))
        mat[pl.ds(pl.multiple_of(up * OWN, OWN), OWN), pl.ds(pl.multiple_of(across * OWN, OWN), OWN)] = tile.astype(
            BF16
        )
        return total + jnp.sum((tile * tile).reshape(OWN // 8, 8, OWN), axis=0)

    total = lax.fori_loop(0, TILES * TILES, assemble, jnp.zeros((8, OWN), F32))

    extra = jnp.zeros((1, OWN), F32)
    start = []
    for tile in range(TILES):
        at = slice(tile * OWN, (tile + 1) * OWN)
        on_diag = jnp.sum(jnp.where(eye, mat[at, at].astype(F32), 0.0), axis=0, keepdims=True)
        energy = diag[:, at]
        extra += energy * (2.0 * on_diag + energy)
        first = 0.5 * (left[:, at] + direct(0, tile))
        if tile == 0:
            first += jnp.where(eye, energy, 0.0)
        start.append(first)
    squares = jnp.sum(jnp.sum(total, axis=0, keepdims=True) + extra, axis=1, keepdims=True)
    scale = jnp.sqrt(active[1, 0] / (4.0 * (squares + 1e-06)))
    energy = diag[...]

    def apply(x):
        high = x.astype(BF16)
        low = (x - high.astype(F32)).astype(BF16)
        y = jnp.dot(jnp.concatenate([high, low], axis=0), mat[...], preferred_element_type=F32)
        return scale * (y[:OWN] + y[OWN:] + x * energy)

    initial = scale * jnp.concatenate(start, axis=1)
    first_step = 1.5 * initial - 0.5 * apply(apply(initial))
    once = apply(first_step)
    once = 1.5 * once - 0.5 * apply(apply(once))
    twice = apply(once)
    twice = 1.5 * twice - 0.5 * apply(apply(twice))
    result = 1.5 * first_step - 0.5 * twice
    for tile in range(TILES):
        at = slice(tile * OWN, (tile + 1) * OWN)
        out[at, :] = result[:, at].T.astype(BF16)


def density_kernel(inverse, sign, inv_tiles, out, placed, sems, local_sem, *bufs):
    def buf(team, oy, oz):
        return bufs[team * SLOTS + oy * 4 + oz]

    row, col, y, z, device = places()
    core = row % 2
    partner = (row + 1 - 2 * core, col)
    across = ((row + 2 * core - 1 + TEAMS) % TEAMS, col)
    near = [device(1, 0), device(3, 0), device(0, 1), device(0, 3), partner, across]
    for ref in bufs:
        ref[MEMBERS] = jnp.zeros((BLOCK, OWN), BF16)
    load = pltpu.make_async_copy(sign, buf(0, 0, 0).at[pl.ds(0, MEMBERS)], local_sem)
    load.start()
    load.wait()
    greet(near)

    def plane(team, rows, first):
        return Gather(
            lambda oy, oz, start, size: buf(team, oy, oz).at[pl.ds(start, size)],
            rows,
            sems.at[0, pl.ds(first, 40)],
            sems.at[1, pl.ds(first, 40)],
            device,
        )

    def onward(team, oy, oz, start, size, n):
        return pltpu.make_async_remote_copy(
            src_ref=buf(0, oy, oz).at[pl.ds(start, size)],
            dst_ref=buf(team, oy, oz).at[pl.ds(start, size)],
            send_sem=sems.at[0, n],
            recv_sem=sems.at[1, n],
            device_id=partner if team == 1 else across,
            device_id_type=MESH,
        )

    def to_partner(oy, oz):
        return onward(1, oy, oz, 0, MEMBERS, 80 + oy * 4 + oz)

    def to_across(oy, oz):
        return onward(2, oy, oz, SHARED, MEMBERS - SHARED, 96 + oy * 4 + oz)

    shared = onward(2, 0, 0, 0, SHARED, 112)
    shared.start()
    mine = plane(0, MEMBERS, 0)
    mine.begin()
    to_across(0, 0).start()
    to_partner(0, 0).start()
    shared.wait_recv()
    theirs = plane(2, SHARED, 40)
    theirs.begin()

    sides = [1, 2 - 2 * core, 2 * core]
    teams = [row, partner[0], across[0]]

    def multiply(team, pair):
        for t, (oy, oz) in enumerate(pair):
            slot = ((y + oy) % 4) * 4 + (z + oz) % 4
            line = teams[team] * SLOTS + slot

            @pl.loop(0, TEAM_BLOCKS // 8)
            def _(i):
                for j in range(8):
                    b = i * 8 + j
                    placed[pl.ds(pl.multiple_of(b * BLOCK, BLOCK), BLOCK), t * OWN : (t + 1) * OWN] = buf(
                        team, oy, oz
                    )[inverse[line, b]]

        side = sides[team]
        result = jnp.dot(inv_tiles[side], placed[...], preferred_element_type=F32)
        for t, (oy, oz) in enumerate(pair):
            slot = ((y + oy) % 4) * 4 + (z + oz) % 4
            out[side, :, pl.ds(pl.multiple_of(slot * OWN, OWN), OWN)] = result[:, t * OWN : (t + 1) * OWN]

    order, order_theirs, ready = [(0, 0)], [(0, 0)], []
    mine_steps, their_steps = mine.steps(), theirs.steps()
    turns = ["mine"] * LEAD + ["theirs", "mine"] * (40 - LEAD) + ["theirs"] * LEAD
    for turn in turns:
        if turn == "mine":
            spot = next(mine_steps)
            if spot:
                order.append(spot)
                to_across(*spot).start()
                to_partner(*spot).start()
                if len(order) % 2 == 0:
                    multiply(0, order[-2:])
                    ready.append(order[-2:])
        else:
            spot = next(their_steps)
            if spot:
                order_theirs.append(spot)
                if len(ready) > 1 or (ready and len(order) == SLOTS):
                    pair = ready.pop(0)
                    for spot in pair:
                        to_partner(*spot).wait_recv()
                    multiply(1, pair)
                if len(order_theirs) % 2 == 0:
                    for spot in order_theirs[-2:]:
                        to_across(*spot).wait_recv()
                    multiply(2, order_theirs[-2:])
    for pair in ready:
        for spot in pair:
            to_partner(*spot).wait_recv()
        multiply(1, pair)
    for last in (mine_steps, their_steps):
        assert next(last, None) is None
    shared.wait_send()
    mine.finish()
    theirs.finish()
    for spot in order:
        to_partner(*spot).wait_send()
        to_across(*spot).wait_send()


def shards(hamiltonian, pattern, onsite, members, orders, intersection_inv):
    smem = pl.BlockSpec(memory_space=pltpu.SMEM)
    vmem = pl.BlockSpec(memory_space=pltpu.VMEM)
    hits = members[:, None, :] == jnp.arange(TEAM_BLOCKS, dtype=jnp.int32)[None, :, None]
    behind = MEMBERS - jnp.arange(MEMBERS, dtype=jnp.int32)
    inverse = MEMBERS - jnp.sum(jnp.where(hits, behind, 0), axis=2)
    row, col = lax.axis_index("row"), lax.axis_index("col")
    group = lax.dynamic_index_in_dim(members, row * SLOTS + col, 0, keepdims=False)
    order = lax.dynamic_index_in_dim(orders, row * SLOTS + col, 0, keepdims=False)
    at = jnp.arange(MEMBERS, dtype=jnp.int32)
    part = group % OWN_BLOCKS
    slot = ((group // 16 - col // 4) % 4) * 4 + (group // OWN_BLOCKS - col) % 4
    turn = (at - part) % 4
    table = jnp.stack([group, slot * 4 + turn, slot, turn * SLOTS + group // OWN_BLOCKS, part])
    active = jnp.stack([(at < order).astype(F32), jnp.full((MEMBERS,), BLOCK, F32) * order.astype(F32)])
    sign = pl.pallas_call(
        sign_kernel,
        out_shape=jax.ShapeDtypeStruct((SUB, OWN), BF16),
        in_specs=[smem, smem, vmem, vmem, vmem],
        out_specs=vmem,
        scratch_shapes=[
            pltpu.VMEM((TEAM_BLOCKS, BLOCK, OWN), F32),
            pltpu.VMEM((4 * SLOTS, 1, OWN), F32),
            pltpu.VMEM((OWN, SUB), F32),
            pltpu.VMEM((SLOTS * 4, TILES, OWN, OWN), BF16),
            pltpu.VMEM((SLOTS, TILES, OWN_BLOCKS, BLOCK, OWN), BF16),
            pltpu.VMEM((SUB, SUB), BF16),
            pltpu.VMEM((1, SUB), F32),
            pltpu.SemaphoreType.DMA((40,)),
            pltpu.SemaphoreType.DMA((40,)),
            *[pltpu.VMEM((TEAM_BLOCKS, BLOCK, OWN), BF16) for _ in range(SLOTS)],
        ],
        compiler_params=pltpu.CompilerParams(
            collective_id=0, has_side_effects=True, vmem_limit_bytes=46 * 1024 * 1024
        ),
        name="sign_step",
    )(table, active, hamiltonian.reshape(TEAM_WIDTH, OWN), pattern.T, onsite.reshape(SLOTS, OWN))
    density = pl.pallas_call(
        density_kernel,
        out_shape=pltpu.VMEM((3, OWN, TEAM_WIDTH), F32),
        in_specs=[smem, pl.BlockSpec(memory_space=pl.ANY), vmem],
        out_specs=vmem,
        scratch_shapes=[
            pltpu.VMEM((TEAM_WIDTH, 2 * OWN), BF16),
            pltpu.SemaphoreType.DMA((2, 113)),
            pltpu.SemaphoreType.DMA,
            *[pltpu.VMEM((MEMBERS + 1, BLOCK, OWN), BF16) for _ in range(3 * SLOTS)],
        ],
        compiler_params=pltpu.CompilerParams(
            collective_id=1, has_side_effects=True, vmem_limit_bytes=40 * 1024 * 1024
        ),
        name="density",
    )(inverse, sign.reshape(MEMBERS, BLOCK, OWN), intersection_inv.transpose(1, 0, 2))
    return density.transpose(1, 0, 2)


def solution(mesh):
    in_specs = (P("row", "col"), P("row", "col"), P("row"), P(), P(), P(("row", "col"), None, None))
    out_specs = P(("row", "col"), None, None)
    return jax.shard_map(shards, mesh=mesh, in_specs=in_specs, out_specs=out_specs, check_vma=False)
```

```python
import jax
import jax.numpy as jnp
from jax import lax
from jax.experimental import pallas as pl
from jax.experimental.pallas import tpu as pltpu
from jax.sharding import PartitionSpec as P

BLOCK = 32
OWN_BLOCKS = 4
MEMBERS = 32
SLOTS = 16
TEAMS = 8
TEAM_BLOCKS = 64
TEAM_WIDTH = 2048
SUB = MEMBERS * BLOCK
OWN = OWN_BLOCKS * BLOCK
TILES = SUB // OWN
F32 = jnp.float32
BF16 = jnp.bfloat16
MESH = pl.DeviceIdType.MESH
SHARED = 12
LEAD = 10
RINGS = ((0, 0), (0, 1), (1, 0), (1, 1), (0, 2), (0, 3), (4, 0), (4, 1), (2, 0), (2, 1))
RINGS += ((1, 2), (1, 3), (3, 0), (3, 1), (4, 2), (4, 3), (2, 2), (2, 3), (3, 2), (3, 3))
FIRST = [half * 20 + ring * 4 + k for ring, k in RINGS for half in (0, 1)]
SECOND = FIRST[:LEAD]
for lag in range(40 - LEAD):
    SECOND += [40 + FIRST[lag], FIRST[LEAD + lag]]
SECOND += [40 + n for n in FIRST[40 - LEAD :]]
RING_K = ((0, 3), (0, 1), (3, 2), (1, 2))


class Gather:
    def __init__(self, region, rows, send_sems, recv_sems, device):
        self.region, self.rows, self.device = region, rows, device
        self.send_sems, self.recv_sems = send_sems, recv_sems
        self.got, self.seen = {(0, 0): {0, 1}}, set()

    def copy(self, half, ring, k):
        source, landing = RING_K[k]
        step = 1 if k in (0, 2) else -1
        rows = self.rows // 2
        start, size = half * rows, rows
        if k >= 2:
            size = rows // 2
            start += size * (k - 2)

        def spot(offset):
            a, b = (offset, 0) if ring == 0 else (ring - 1, offset)
            return (b, a) if half == 0 else (a, b)

        along_z = (half == 0) == (ring == 0)
        n = half * 20 + ring * 4 + k
        return pltpu.make_async_remote_copy(
            src_ref=self.region(*spot(source), start, size),
            dst_ref=self.region(*spot(landing), start, size),
            send_sem=self.send_sems.at[n],
            recv_sem=self.recv_sems.at[n],
            device_id=self.device(0, step) if along_z else self.device(step, 0),
            device_id_type=MESH,
        ), spot(landing)

    def begin(self):
        for ring in (0, 1):
            for half in (0, 1):
                for k in (0, 1):
                    self.copy(half, ring, k)[0].start()

    def arrive(self, half, ring, k):
        copy, spot = self.copy(half, ring, k)
        copy.wait_recv()
        if k < 2:
            self.copy(half, ring, k + 2)[0].start()
        self.seen.add((half, ring, k))
        if k >= 2 and (half, ring, 5 - k) not in self.seen:
            return None, False
        if ring == 0:
            for j in (0, 1):
                self.copy(half, RING_K[k][1] + 1, j)[0].start()
        halves = self.got.setdefault(spot, set())
        halves.add(half)
        return spot, len(halves) == 2

    def finish(self):
        for half in (0, 1):
            for ring in range(5):
                for k in range(4):
                    self.copy(half, ring, k)[0].wait_send()


def places():
    row, col = lax.axis_index("row"), lax.axis_index("col")
    y, z = col // 4, col % 4

    def device(dy, dz):
        return (row, ((y + dy + 4) % 4) * 4 + (z + dz + 4) % 4)

    return row, col, y, z, device


def kernel(
    table, active, inverse, ham_in, pattern, onsite, inv_in, out,
    ham, inv_tiles, own, onsites, left, rolled, turned, mat, diag, placed, local_sems, sems, *scratch
):
    row, col, y, z, device = places()
    group = row * SLOTS + col
    core = row % 2
    partner = (row + 1 - 2 * core, col)
    across = ((row + 2 * core - 1 + TEAMS) % TEAMS, col)
    near = [device(1, 0), device(3, 0), device(0, 1), device(0, 3), partner, across]
    barrier = pltpu.get_barrier_semaphore()
    for one in near:
        pl.semaphore_signal(barrier, inc=1, device_id=one, device_id_type=MESH)
    ham_load = pltpu.make_async_copy(ham_in, ham, local_sems.at[0])
    inv_load = pltpu.make_async_copy(inv_in, inv_tiles, local_sems.at[1])
    ham_load.start()
    inv_load.start()
    bufs, signs = scratch[:SLOTS], scratch[SLOTS:]
    for ref in signs:
        ref[MEMBERS] = jnp.zeros((BLOCK, OWN), BF16)
    lanes = lax.broadcasted_iota(jnp.int32, (OWN_BLOCKS, OWN), 1) // BLOCK
    spread = (lanes == lax.broadcasted_iota(jnp.int32, (OWN_BLOCKS, OWN), 0)).astype(F32)
    weights = lax.dot_general(
        pattern[...].astype(F32), spread, (((0,), (0,)), ((), ())), preferred_element_type=F32
    )
    ham_load.wait()
    for a in range(TEAM_BLOCKS):
        masked = ham[a * BLOCK : (a + 1) * BLOCK, :] * weights[a : a + 1, :]
        own[a] = masked
        bufs[0][a] = masked.astype(BF16)
    pl.semaphore_wait(barrier, len(near))

    def plane(region, rows, first):
        return Gather(region, rows, sems.at[0, pl.ds(first, 40)], sems.at[1, pl.ds(first, 40)], device)

    gather = plane(lambda oy, oz, start, size: bufs[oy * 4 + oz].at[pl.ds(start, size)], TEAM_BLOCKS, 0)
    gather.begin()
    for s in range(4):
        onsites[s * SLOTS : (s + 1) * SLOTS] = pltpu.roll(onsite[...], s * BLOCK, axis=1).reshape(SLOTS, 1, OWN)
    one_row = lax.broadcasted_iota(jnp.int32, (1, OWN), 1) // BLOCK

    def blocks(read, tile):
        pieces = [read(table[0, tile * 4 + q, group]).astype(F32) * active[tile * 4 + q, group] for q in range(4)]
        return jnp.concatenate(pieces, axis=0)

    @pl.loop(0, TILES)
    def _(tile):
        at = pl.ds(pl.multiple_of(tile * OWN, OWN), OWN)
        left[:, at] = blocks(lambda m: own[m], tile).T
        picked = jnp.zeros((1, OWN), F32)
        for q in range(4):
            line = onsites[table[3, tile * 4 + q, group]] * active[tile * 4 + q, group]
            picked = jnp.where(one_row == q, line, picked)
        diag[:, at] = picked

    def take_in(oy, oz):
        slot = oy * 4 + oz

        @pl.loop(0, TILES)
        def _(tile):
            x = blocks(lambda m: bufs[slot][m], tile)
            turned[slot, tile] = x.T.astype(BF16).reshape(4, BLOCK, OWN)
            rolled[slot * 4, tile] = x.astype(BF16)
            for s in (1, 2, 3):
                rolled[slot * 4 + s, tile] = pltpu.roll(x, s * BLOCK, axis=1).astype(BF16)

    take_in(0, 0)
    for n in FIRST:
        spot, whole = gather.arrive(n // 20, n % 20 // 4, n % 4)
        if whole:
            take_in(*spot)

    which = lax.broadcasted_iota(jnp.int32, (OWN, OWN), 1) // BLOCK
    eye = lax.broadcasted_iota(jnp.int32, (OWN, OWN), 0) == lax.broadcasted_iota(jnp.int32, (OWN, OWN), 1)

    def direct(up, over):
        tile = None
        for q in range(4):
            piece = rolled[table[1, over * 4 + q, group], up].astype(F32) * active[over * 4 + q, group]
            tile = piece if tile is None else jnp.where(which == q, piece, tile)
        return tile

    def mirrored(up, over):
        pieces = []
        for q in range(4):
            a = up * 4 + q
            pieces.append(turned[table[2, a, group], over, table[4, a, group]].astype(F32) * active[a, group])
        return jnp.concatenate(pieces, axis=0)

    def assemble(n, total):
        up, over = n // TILES, n % TILES
        tile = 0.5 * (direct(up, over) + mirrored(up, over))
        mat[pl.ds(pl.multiple_of(up * OWN, OWN), OWN), pl.ds(pl.multiple_of(over * OWN, OWN), OWN)] = tile.astype(
            BF16
        )
        return total + jnp.sum((tile * tile).reshape(OWN // 8, 8, OWN), axis=0)

    total = lax.fori_loop(0, TILES * TILES, assemble, jnp.zeros((8, OWN), F32))

    extra = jnp.zeros((1, OWN), F32)
    start = []
    for tile in range(TILES):
        at = slice(tile * OWN, (tile + 1) * OWN)
        on_diag = jnp.sum(jnp.where(eye, mat[at, at].astype(F32), 0.0), axis=0, keepdims=True)
        energy = diag[:, at]
        extra += energy * (2.0 * on_diag + energy)
        first = 0.5 * (left[:, at] + direct(0, tile))
        if tile == 0:
            first += jnp.where(eye, energy, 0.0)
        start.append(first)
    count = 0.0
    for a in range(MEMBERS):
        count += active[a, group] * float(BLOCK)
    squares = jnp.sum(jnp.sum(total, axis=0, keepdims=True) + extra, axis=1, keepdims=True)
    scale = jnp.sqrt(count / (4.0 * (squares + 1e-06)))
    energy = diag[...]

    def apply(x):
        high = x.astype(BF16)
        low = (x - high.astype(F32)).astype(BF16)
        y = jnp.dot(jnp.concatenate([high, low], axis=0), mat[...], preferred_element_type=F32)
        return scale * (y[:OWN] + y[OWN:] + x * energy)

    initial = scale * jnp.concatenate(start, axis=1)
    first_step = 1.5 * initial - 0.5 * apply(apply(initial))
    once = apply(first_step)
    once = 1.5 * once - 0.5 * apply(apply(once))
    twice = apply(once)
    twice = 1.5 * twice - 0.5 * apply(apply(twice))
    result = 1.5 * first_step - 0.5 * twice
    for tile in range(TILES):
        turned_back = result[:, tile * OWN : (tile + 1) * OWN].T.astype(BF16)
        signs[0][tile * 4 : (tile + 1) * 4] = turned_back.reshape(4, BLOCK, OWN)
    gather.finish()
    inv_load.wait()

    def sign_at(team, oy, oz):
        return signs[team * SLOTS + oy * 4 + oz]

    def onward(team, oy, oz, start, size, n):
        return pltpu.make_async_remote_copy(
            src_ref=sign_at(0, oy, oz).at[pl.ds(start, size)],
            dst_ref=sign_at(team, oy, oz).at[pl.ds(start, size)],
            send_sem=sems.at[0, n],
            recv_sem=sems.at[1, n],
            device_id=partner if team == 1 else across,
            device_id_type=MESH,
        )

    def to_partner(oy, oz):
        return onward(1, oy, oz, 0, MEMBERS, 120 + oy * 4 + oz)

    def to_across(oy, oz, half):
        start = half * MEMBERS // 2 + SHARED // 2
        return onward(2, oy, oz, start, (MEMBERS - SHARED) // 2, 136 + half * SLOTS + oy * 4 + oz)

    shared = [onward(2, 0, 0, half * MEMBERS // 2, SHARED // 2, 168 + half) for half in (0, 1)]
    for half in (0, 1):
        shared[half].start()
    mine = plane(lambda oy, oz, start, size: sign_at(0, oy, oz).at[pl.ds(start, size)], MEMBERS, 40)
    mine.begin()
    for half in (0, 1):
        to_across(0, 0, half).start()
    to_partner(0, 0).start()
    for half in (0, 1):
        shared[half].wait_recv()

    def shared_part(oy, oz, start, size):
        half = start // (SHARED // 2)
        return sign_at(2, oy, oz).at[pl.ds(half * MEMBERS // 2 + start % (SHARED // 2), size)]

    theirs = plane(shared_part, SHARED, 80)
    theirs.begin()

    sides = [1, 2 - 2 * core, 2 * core]
    teams = [row, partner[0], across[0]]

    def multiply(team, pair):
        for t, (oy, oz) in enumerate(pair):
            slot = ((y + oy) % 4) * 4 + (z + oz) % 4
            line = teams[team] * SLOTS + slot

            @pl.loop(0, TEAM_BLOCKS // 8)
            def _(i):
                for j in range(8):
                    b = i * 8 + j
                    placed[pl.ds(pl.multiple_of(b * BLOCK, BLOCK), BLOCK), t * OWN : (t + 1) * OWN] = sign_at(
                        team, oy, oz
                    )[inverse[line, b]]

        side = sides[team]
        result = jnp.dot(inv_tiles[side], placed[...], preferred_element_type=F32)
        for t, (oy, oz) in enumerate(pair):
            slot = ((y + oy) % 4) * 4 + (z + oz) % 4
            out[side, :, pl.ds(pl.multiple_of(slot * OWN, OWN), OWN)] = result[:, t * OWN : (t + 1) * OWN]

    order, order_theirs, ready = [(0, 0)], [(0, 0)], []
    for n in SECOND:
        half, ring, k = n % 40 // 20, n % 20 // 4, n % 4
        spot, whole = (mine if n < 40 else theirs).arrive(half, ring, k)
        if n < 40 and spot:
            to_across(*spot, half).start()
        if not whole:
            continue
        if n < 40:
            order.append(spot)
            to_partner(*spot).start()
            if len(order) % 2 == 0:
                multiply(0, order[-2:])
                ready.append(order[-2:])
        else:
            order_theirs.append(spot)
            if len(ready) > 1 or (ready and len(order) == SLOTS):
                pair = ready.pop(0)
                for one in pair:
                    to_partner(*one).wait_recv()
                multiply(1, pair)
            if len(order_theirs) % 2 == 0:
                for one in order_theirs[-2:]:
                    to_across(*one, 0).wait_recv()
                    to_across(*one, 1).wait_recv()
                multiply(2, order_theirs[-2:])
    for pair in ready:
        for one in pair:
            to_partner(*one).wait_recv()
        multiply(1, pair)
    mine.finish()
    theirs.finish()
    for half in (0, 1):
        shared[half].wait_send()
        for one in order:
            to_across(*one, half).wait_send()
    for one in order:
        to_partner(*one).wait_send()


def shards(hamiltonian, pattern, onsite, members, orders, intersection_inv):
    smem = pl.BlockSpec(memory_space=pltpu.SMEM)
    vmem = pl.BlockSpec(memory_space=pltpu.VMEM)
    hbm = pl.BlockSpec(memory_space=pl.ANY)
    across = members.T
    hits = across[:, :, None] == jnp.arange(TEAM_BLOCKS, dtype=jnp.int32)
    behind = MEMBERS - jnp.arange(MEMBERS, dtype=jnp.int32)
    inverse = MEMBERS - jnp.sum(jnp.where(hits, behind[:, None, None], 0), axis=0)
    col = lax.axis_index("col")
    which = lax.broadcasted_iota(jnp.int32, (5, MEMBERS, TEAMS * SLOTS), 0)
    at = lax.broadcasted_iota(jnp.int32, (MEMBERS, TEAMS * SLOTS), 0)
    part, block = across & 3, across >> 2
    slot = (((block >> 2) - (col >> 2)) & 3) * 4 + ((block - col) & 3)
    turn = (at - part) & 3
    table = part
    for n, values in enumerate((across, slot * 4 + turn, slot, turn * SLOTS + block)):
        table = jnp.where(which == n, values, table)
    active = (at < orders).astype(F32)
    density = pl.pallas_call(
        kernel,
        out_shape=pltpu.VMEM((3, OWN, TEAM_WIDTH), F32),
        in_specs=[smem, smem, smem, hbm, vmem, vmem, hbm],
        out_specs=vmem,
        scratch_shapes=[
            pltpu.VMEM((TEAM_WIDTH, OWN), F32),
            pltpu.VMEM((3, OWN, TEAM_WIDTH), BF16),
            pltpu.VMEM((TEAM_BLOCKS, BLOCK, OWN), F32),
            pltpu.VMEM((4 * SLOTS, 1, OWN), F32),
            pltpu.VMEM((OWN, SUB), F32),
            pltpu.VMEM((SLOTS * 4, TILES, OWN, OWN), BF16),
            pltpu.VMEM((SLOTS, TILES, OWN_BLOCKS, BLOCK, OWN), BF16),
            pltpu.VMEM((SUB, SUB), BF16),
            pltpu.VMEM((1, SUB), F32),
            pltpu.VMEM((TEAM_WIDTH, 2 * OWN), BF16),
            pltpu.SemaphoreType.DMA((2,)),
            pltpu.SemaphoreType.DMA((2, 170)),
            *[pltpu.VMEM((TEAM_BLOCKS, BLOCK, OWN), BF16) for _ in range(SLOTS)],
            *[pltpu.VMEM((MEMBERS + 1, BLOCK, OWN), BF16) for _ in range(3 * SLOTS)],
        ],
        compiler_params=pltpu.CompilerParams(
            collective_id=0, has_side_effects=True, vmem_limit_bytes=56 * 1024 * 1024
        ),
        name="density",
    )(table, active, inverse, hamiltonian, pattern.T, onsite.reshape(SLOTS, OWN), intersection_inv.transpose(1, 0, 2))
    return density.transpose(1, 0, 2)


def solution(mesh):
    in_specs = (P("row", "col"), P("row", "col"), P("row"), P(), P(), P(("row", "col"), None, None))
    out_specs = P(("row", "col"), None, None)
    return jax.shard_map(shards, mesh=mesh, in_specs=in_specs, out_specs=out_specs, check_vma=False)
```

```python
import jax
import jax.numpy as jnp
from jax import lax
from jax.experimental import pallas as pl
from jax.experimental.pallas import tpu as pltpu
from jax.sharding import PartitionSpec as P

BLOCK = 32
OWN_BLOCKS = 4
MEMBERS = 32
SLOTS = 16
TEAMS = 8
TEAM_BLOCKS = 64
TEAM_WIDTH = 2048
SUB = MEMBERS * BLOCK
OWN = OWN_BLOCKS * BLOCK
TILES = SUB // OWN
F32 = jnp.float32
BF16 = jnp.bfloat16
MESH = pl.DeviceIdType.MESH
SHARED = 12
LEAD = 10
LAG = 4
UNITS = 1
RINGS = ((0, 0), (0, 1), (1, 0), (1, 1), (0, 2), (0, 3), (4, 0), (4, 1), (2, 0), (2, 1))
RINGS += ((1, 2), (1, 3), (3, 0), (3, 1), (4, 2), (4, 3), (2, 2), (2, 3), (3, 2), (3, 3))
FIRST = [half * 20 + ring * 4 + k for ring, k in RINGS for half in (0, 1)]
SECOND = FIRST[:LEAD]
for lag in range(40 - LEAD):
    SECOND += [40 + FIRST[lag], FIRST[LEAD + lag]]
SECOND += [40 + n for n in FIRST[40 - LEAD :]]
RING_K = ((0, 3), (0, 1), (3, 2), (1, 2))


class Gather:
    def __init__(self, region, rows, send_sems, recv_sems, device):
        self.region, self.rows, self.device = region, rows, device
        self.send_sems, self.recv_sems = send_sems, recv_sems
        self.got, self.seen = {(0, 0): {0, 1}}, set()

    def copy(self, half, ring, k):
        source, landing = RING_K[k]
        step = 1 if k in (0, 2) else -1
        rows = self.rows // 2
        start, size = half * rows, rows
        if k >= 2:
            size = rows // 2
            start += size * (k - 2)

        def spot(offset):
            a, b = (offset, 0) if ring == 0 else (ring - 1, offset)
            return (b, a) if half == 0 else (a, b)

        along_z = (half == 0) == (ring == 0)
        n = half * 20 + ring * 4 + k
        return pltpu.make_async_remote_copy(
            src_ref=self.region(*spot(source), start, size),
            dst_ref=self.region(*spot(landing), start, size),
            send_sem=self.send_sems.at[n],
            recv_sem=self.recv_sems.at[n],
            device_id=self.device(0, step) if along_z else self.device(step, 0),
            device_id_type=MESH,
        ), spot(landing)

    def begin(self):
        for ring in (0, 1):
            for half in (0, 1):
                for k in (0, 1):
                    self.copy(half, ring, k)[0].start()

    def arrive(self, half, ring, k):
        copy, spot = self.copy(half, ring, k)
        copy.wait_recv()
        if k < 2:
            self.copy(half, ring, k + 2)[0].start()
        self.seen.add((half, ring, k))
        if k >= 2 and (half, ring, 5 - k) not in self.seen:
            return None, False
        if ring == 0:
            for j in (0, 1):
                self.copy(half, RING_K[k][1] + 1, j)[0].start()
        halves = self.got.setdefault(spot, set())
        halves.add(half)
        return spot, len(halves) == 2

    def finish(self):
        for half in (0, 1):
            for ring in range(5):
                for k in range(4):
                    self.copy(half, ring, k)[0].wait_send()


def places():
    row, col = lax.axis_index("row"), lax.axis_index("col")
    y, z = col // 4, col % 4

    def device(dy, dz):
        return (row, ((y + dy + 4) % 4) * 4 + (z + dz + 4) % 4)

    return row, col, y, z, device


def kernel(
    listed, rolled_at, slot_at, onsite_at, part_at, active, inverse, ham_in, pattern, onsite, inv_in, out,
    ham, inv_tiles, own, onsites, left, rolled, turned, mat, diag, placed, local_sems, sems, *scratch
):
    row, col, y, z, device = places()
    group = row * SLOTS + col
    core = row % 2
    partner = (row + 1 - 2 * core, col)
    across = ((row + 2 * core - 1 + TEAMS) % TEAMS, col)
    near = [device(1, 0), device(3, 0), device(0, 1), device(0, 3), partner, across]
    barrier = pltpu.get_barrier_semaphore()
    for one in near:
        pl.semaphore_signal(barrier, inc=1, device_id=one, device_id_type=MESH)
    ham_load = pltpu.make_async_copy(ham_in, ham, local_sems.at[0])
    inv_load = pltpu.make_async_copy(inv_in, inv_tiles, local_sems.at[1])
    ham_load.start()
    inv_load.start()
    bufs, signs = scratch[:SLOTS], scratch[SLOTS:]
    for ref in signs:
        ref[0] = jnp.zeros((BLOCK, OWN), BF16)
    lanes = lax.broadcasted_iota(jnp.int32, (OWN_BLOCKS, OWN), 1) // BLOCK
    spread = (lanes == lax.broadcasted_iota(jnp.int32, (OWN_BLOCKS, OWN), 0)).astype(F32)
    weights = lax.dot_general(
        pattern[...].astype(F32), spread, (((0,), (0,)), ((), ())), preferred_element_type=F32
    )
    ham_load.wait()
    for a in range(TEAM_BLOCKS):
        masked = ham[a * BLOCK : (a + 1) * BLOCK, :] * weights[a : a + 1, :]
        own[a] = masked
        bufs[0][a] = masked.astype(BF16)
    pl.semaphore_wait(barrier, len(near))

    def plane(region, rows, first):
        return Gather(region, rows, sems.at[0, pl.ds(first, 40)], sems.at[1, pl.ds(first, 40)], device)

    gather = plane(lambda oy, oz, start, size: bufs[oy * 4 + oz].at[pl.ds(start, size)], TEAM_BLOCKS, 0)
    gather.begin()
    for s in range(4):
        onsites[s * SLOTS : (s + 1) * SLOTS] = pltpu.roll(onsite[...], s * BLOCK, axis=1).reshape(SLOTS, 1, OWN)
    one_row = lax.broadcasted_iota(jnp.int32, (1, OWN), 1) // BLOCK

    def blocks(read, tile):
        pieces = [read(listed[tile * 4 + q, group]).astype(F32) * active[tile * 4 + q, group] for q in range(4)]
        return jnp.concatenate(pieces, axis=0)

    @pl.loop(0, TILES)
    def _(tile):
        at = pl.ds(pl.multiple_of(tile * OWN, OWN), OWN)
        left[:, at] = blocks(lambda m: own[m], tile).T
        picked = jnp.zeros((1, OWN), F32)
        for q in range(4):
            line = onsites[onsite_at[tile * 4 + q, group]] * active[tile * 4 + q, group]
            picked = jnp.where(one_row == q, line, picked)
        diag[:, at] = picked

    def take_in(oy, oz):
        slot = oy * 4 + oz

        @pl.loop(0, TILES)
        def _(tile):
            x = blocks(lambda m: bufs[slot][m], tile)
            turned[slot, tile] = x.T.astype(BF16).reshape(4, BLOCK, OWN)
            rolled[slot * 4, tile] = x.astype(BF16)
            for s in (1, 2, 3):
                rolled[slot * 4 + s, tile] = pltpu.roll(x, s * BLOCK, axis=1).astype(BF16)

    take_in(0, 0)
    for n in FIRST:
        spot, whole = gather.arrive(n // 20, n % 20 // 4, n % 4)
        if whole:
            take_in(*spot)

    which = lax.broadcasted_iota(jnp.int32, (OWN, OWN), 1) // BLOCK
    eye = lax.broadcasted_iota(jnp.int32, (OWN, OWN), 0) == lax.broadcasted_iota(jnp.int32, (OWN, OWN), 1)

    def direct(up, over):
        tile = None
        for q in range(4):
            piece = rolled[rolled_at[over * 4 + q, group], up].astype(F32) * active[over * 4 + q, group]
            tile = piece if tile is None else jnp.where(which == q, piece, tile)
        return tile

    def mirrored(up, over):
        pieces = []
        for q in range(4):
            a = up * 4 + q
            pieces.append(turned[slot_at[a, group], over, part_at[a, group]].astype(F32) * active[a, group])
        return jnp.concatenate(pieces, axis=0)

    def assemble(n, total):
        up, over = n // TILES, n % TILES
        tile = 0.5 * (direct(up, over) + mirrored(up, over))
        mat[pl.ds(pl.multiple_of(up * OWN, OWN), OWN), pl.ds(pl.multiple_of(over * OWN, OWN), OWN)] = tile.astype(
            BF16
        )
        return total + jnp.sum((tile * tile).reshape(OWN // 8, 8, OWN), axis=0)

    total = lax.fori_loop(0, TILES * TILES, assemble, jnp.zeros((8, OWN), F32))

    extra = jnp.zeros((1, OWN), F32)
    start = []
    for tile in range(TILES):
        at = slice(tile * OWN, (tile + 1) * OWN)
        on_diag = jnp.sum(jnp.where(eye, mat[at, at].astype(F32), 0.0), axis=0, keepdims=True)
        energy = diag[:, at]
        extra += energy * (2.0 * on_diag + energy)
        first = 0.5 * (left[:, at] + direct(0, tile))
        if tile == 0:
            first += jnp.where(eye, energy, 0.0)
        start.append(first)
    count = 0.0
    for a in range(MEMBERS):
        count += active[a, group] * float(BLOCK)
    squares = jnp.sum(jnp.sum(total, axis=0, keepdims=True) + extra, axis=1, keepdims=True)
    scale = jnp.sqrt(count / (4.0 * (squares + 1e-06)))
    energy = diag[...]

    def apply(x):
        high = x.astype(BF16)
        low = (x - high.astype(F32)).astype(BF16)
        y = jnp.dot(jnp.concatenate([high, low], axis=0), mat[...], preferred_element_type=F32)
        return scale * (y[:OWN] + y[OWN:] + x * energy)

    initial = scale * jnp.concatenate(start, axis=1)
    first_step = 1.5 * initial - 0.5 * apply(apply(initial))
    once = apply(first_step)
    once = 1.5 * once - 0.5 * apply(apply(once))
    twice = apply(once)
    twice = 1.5 * twice - 0.5 * apply(apply(twice))
    result = 1.5 * first_step - 0.5 * twice
    for tile in range(TILES):
        turned_back = result[:, tile * OWN : (tile + 1) * OWN].T.astype(BF16)
        signs[0][tile * 4 + 1 : tile * 4 + 5] = turned_back.reshape(4, BLOCK, OWN)
    gather.finish()
    inv_load.wait()

    def sign_at(team, oy, oz):
        return signs[team * SLOTS + oy * 4 + oz]

    def onward(team, oy, oz, start, size, n):
        return pltpu.make_async_remote_copy(
            src_ref=sign_at(0, oy, oz).at[pl.ds(start + 1, size)],
            dst_ref=sign_at(team, oy, oz).at[pl.ds(start + 1, size)],
            send_sem=sems.at[0, n],
            recv_sem=sems.at[1, n],
            device_id=partner if team == 1 else across,
            device_id_type=MESH,
        )

    def to_partner(oy, oz):
        return onward(1, oy, oz, 0, MEMBERS, 120 + oy * 4 + oz)

    def to_across(oy, oz, half):
        start = half * MEMBERS // 2 + SHARED // 2
        return onward(2, oy, oz, start, (MEMBERS - SHARED) // 2, 136 + half * SLOTS + oy * 4 + oz)

    shared = [onward(2, 0, 0, half * MEMBERS // 2, SHARED // 2, 168 + half) for half in (0, 1)]
    for half in (0, 1):
        shared[half].start()
    mine = plane(lambda oy, oz, start, size: sign_at(0, oy, oz).at[pl.ds(start + 1, size)], MEMBERS, 40)
    mine.begin()
    for half in (0, 1):
        to_across(0, 0, half).start()
    to_partner(0, 0).start()
    for half in (0, 1):
        shared[half].wait_recv()

    def shared_part(oy, oz, start, size):
        half = start // (SHARED // 2)
        return sign_at(2, oy, oz).at[pl.ds(half * MEMBERS // 2 + start % (SHARED // 2) + 1, size)]

    theirs = plane(shared_part, SHARED, 80)
    theirs.begin()

    sides = [1, 2 - 2 * core, 2 * core]
    teams = [row, partner[0], across[0]]

    def place(team, spot, t):
        slot = ((y + spot[0]) % 4) * 4 + (z + spot[1]) % 4
        line = teams[team] * SLOTS + slot

        @pl.loop(0, TEAM_BLOCKS // 16)
        def _(i):
            for j in range(16):
                b = i * 16 + j
                rows = pl.ds(pl.multiple_of(b * BLOCK, BLOCK), BLOCK)
                placed[rows, t * OWN : (t + 1) * OWN] = sign_at(team, *spot)[inverse[b, line]]

    def multiply(team, pair):
        side = sides[team]
        result = jnp.dot(inv_tiles[side], placed[...], preferred_element_type=F32)
        for t, (oy, oz) in enumerate(pair):
            slot = ((y + oy) % 4) * 4 + (z + oz) % 4
            out[side, :, pl.ds(pl.multiple_of(slot * OWN, OWN), OWN)] = result[:, t * OWN : (t + 1) * OWN]

    def work(team, pair):
        for t, spot in enumerate(pair):
            if team == 1:
                to_partner(*spot).wait_recv()
            if team == 2:
                to_across(*spot, 0).wait_recv()
                to_across(*spot, 1).wait_recv()
            place(team, spot, t)
            yield
        multiply(team, pair)
        yield

    order, order_theirs, todo = [(0, 0)], [(0, 0)], []
    for n in SECOND:
        half, ring, k = n % 40 // 20, n % 20 // 4, n % 4
        spot, whole = (mine if n < 40 else theirs).arrive(half, ring, k)
        if n < 40 and spot:
            to_across(*spot, half).start()
        if n < 40 and whole:
            order.append(spot)
            to_partner(*spot).start()
            if len(order) % 2 == 0:
                todo.append(work(0, order[-2:]))
                if len(order) > 2:
                    todo.append(work(1, order[-4:-2]))
            if len(order) == SLOTS:
                todo.append(work(1, order[-2:]))
        if n >= 40 and whole:
            order_theirs.append(spot)
            at = len(order_theirs) - LAG
            if at > 0 and at % 2 == 0:
                todo.append(work(2, order_theirs[at - 2 : at]))
        for _ in range(UNITS):
            while todo and next(todo[0], "end") == "end":
                todo.pop(0)
    for at in range(SLOTS - LAG, SLOTS, 2):
        todo.append(work(2, order_theirs[at : at + 2]))
    for steps in todo:
        for _ in steps:
            pass
    mine.finish()
    theirs.finish()
    for half in (0, 1):
        shared[half].wait_send()
        for one in order:
            to_across(*one, half).wait_send()
    for one in order:
        to_partner(*one).wait_send()


def shards(hamiltonian, pattern, onsite, members, orders, intersection_inv):
    smem = pl.BlockSpec(memory_space=pltpu.SMEM)
    vmem = pl.BlockSpec(memory_space=pltpu.VMEM)
    hbm = pl.BlockSpec(memory_space=pl.ANY)
    listed = members.T
    places_of = lax.broadcasted_iota(jnp.int32, (MEMBERS, TEAM_BLOCKS, TEAMS * SLOTS), 0) + 1
    hits = listed[:, None, :] == lax.broadcasted_iota(jnp.int32, places_of.shape, 1)
    inverse = jnp.sum(jnp.where(hits, places_of, 0), axis=0)
    col = lax.axis_index("col")
    at = lax.broadcasted_iota(jnp.int32, (MEMBERS, TEAMS * SLOTS), 0)
    part, block = listed & 3, listed >> 2
    slot = (((block >> 2) - (col >> 2)) & 3) * 4 + ((block - col) & 3)
    turn = (at - part) & 3
    active = (at < orders).astype(F32)
    density = pl.pallas_call(
        kernel,
        out_shape=pltpu.VMEM((3, OWN, TEAM_WIDTH), F32),
        in_specs=[smem] * 7 + [hbm, vmem, vmem, hbm],
        out_specs=vmem,
        scratch_shapes=[
            pltpu.VMEM((TEAM_WIDTH, OWN), F32),
            pltpu.VMEM((3, OWN, TEAM_WIDTH), BF16),
            pltpu.VMEM((TEAM_BLOCKS, BLOCK, OWN), F32),
            pltpu.VMEM((4 * SLOTS, 1, OWN), F32),
            pltpu.VMEM((OWN, SUB), F32),
            pltpu.VMEM((SLOTS * 4, TILES, OWN, OWN), BF16),
            pltpu.VMEM((SLOTS, TILES, OWN_BLOCKS, BLOCK, OWN), BF16),
            pltpu.VMEM((SUB, SUB), BF16),
            pltpu.VMEM((1, SUB), F32),
            pltpu.VMEM((TEAM_WIDTH, 2 * OWN), BF16),
            pltpu.SemaphoreType.DMA((2,)),
            pltpu.SemaphoreType.DMA((2, 170)),
            *[pltpu.VMEM((TEAM_BLOCKS, BLOCK, OWN), BF16) for _ in range(SLOTS)],
            *[pltpu.VMEM((MEMBERS + 1, BLOCK, OWN), BF16) for _ in range(3 * SLOTS)],
        ],
        compiler_params=pltpu.CompilerParams(
            collective_id=0, has_side_effects=True, vmem_limit_bytes=56 * 1024 * 1024
        ),
        name="density",
    )(
        listed,
        slot * 4 + turn,
        slot,
        turn * SLOTS + block,
        part,
        active,
        inverse,
        hamiltonian,
        pattern.T,
        onsite.reshape(SLOTS, OWN),
        intersection_inv.transpose(1, 0, 2),
    )
    return density.transpose(1, 0, 2)


def solution(mesh):
    in_specs = (P("row", "col"), P("row", "col"), P("row"), P(), P(), P(("row", "col"), None, None))
    out_specs = P(("row", "col"), None, None)
    return jax.shard_map(shards, mesh=mesh, in_specs=in_specs, out_specs=out_specs, check_vma=False)
```

```python
import jax
import jax.numpy as jnp
from jax import lax
from jax.experimental import pallas as pl
from jax.experimental.pallas import tpu as pltpu
from jax.sharding import PartitionSpec as P

BLOCK = 32
OWN_BLOCKS = 4
MEMBERS = 32
SLOTS = 16
TEAMS = 8
TEAM_BLOCKS = 64
TEAM_WIDTH = 2048
SUB = MEMBERS * BLOCK
OWN = OWN_BLOCKS * BLOCK
TILES = SUB // OWN
F32 = jnp.float32
BF16 = jnp.bfloat16
MESH = pl.DeviceIdType.MESH
SHARED = 12
LEAD = 10
LAG = 4
UNITS = 1
RINGS = ((0, 0), (0, 1), (1, 0), (1, 1), (0, 2), (0, 3), (4, 0), (4, 1), (2, 0), (2, 1))
RINGS += ((1, 2), (1, 3), (3, 0), (3, 1), (4, 2), (4, 3), (2, 2), (2, 3), (3, 2), (3, 3))
FIRST = [half * 20 + ring * 4 + k for ring, k in RINGS for half in (0, 1)]
SECOND = FIRST[:LEAD]
for lag in range(40 - LEAD):
    SECOND += [40 + FIRST[lag], FIRST[LEAD + lag]]
SECOND += [40 + n for n in FIRST[40 - LEAD :]]
RING_K = ((0, 3), (0, 1), (3, 2), (1, 2))


class Gather:
    def __init__(self, region, rows, send_sems, recv_sems, device):
        self.region, self.rows, self.device = region, rows, device
        self.send_sems, self.recv_sems = send_sems, recv_sems
        self.got, self.seen = {(0, 0): {0, 1}}, set()

    def copy(self, half, ring, k):
        source, landing = RING_K[k]
        step = 1 if k in (0, 2) else -1
        rows = self.rows // 2
        start, size = half * rows, rows
        if k >= 2:
            size = rows // 2
            start += size * (k - 2)

        def spot(offset):
            a, b = (offset, 0) if ring == 0 else (ring - 1, offset)
            return (b, a) if half == 0 else (a, b)

        along_z = (half == 0) == (ring == 0)
        n = half * 20 + ring * 4 + k
        return pltpu.make_async_remote_copy(
            src_ref=self.region(*spot(source), start, size),
            dst_ref=self.region(*spot(landing), start, size),
            send_sem=self.send_sems.at[n],
            recv_sem=self.recv_sems.at[n],
            device_id=self.device(0, step) if along_z else self.device(step, 0),
            device_id_type=MESH,
        ), spot(landing)

    def begin(self):
        for ring in (0, 1):
            for half in (0, 1):
                for k in (0, 1):
                    self.copy(half, ring, k)[0].start()

    def arrive(self, half, ring, k):
        copy, spot = self.copy(half, ring, k)
        copy.wait_recv()
        if k < 2:
            self.copy(half, ring, k + 2)[0].start()
        self.seen.add((half, ring, k))
        if k >= 2 and (half, ring, 5 - k) not in self.seen:
            return None, False
        if ring == 0:
            for j in (0, 1):
                self.copy(half, RING_K[k][1] + 1, j)[0].start()
        halves = self.got.setdefault(spot, set())
        halves.add(half)
        return spot, len(halves) == 2

    def finish(self):
        for half in (0, 1):
            for ring in range(5):
                for k in range(4):
                    self.copy(half, ring, k)[0].wait_send()


def places():
    row, col = lax.axis_index("row"), lax.axis_index("col")
    y, z = col // 4, col % 4

    def device(dy, dz):
        return (row, ((y + dy + 4) % 4) * 4 + (z + dz + 4) % 4)

    return row, col, y, z, device


def kernel(
    listed, rolled_at, slot_at, onsite_at, part_at, orders, inverse, ham_in, pattern, onsite, inv_in, out,
    ham, inv_tiles, own, onsites, left, rolled, turned, mat, diag, placed, local_sems, sems, *scratch
):
    row, col, y, z, device = places()
    group = row * SLOTS + col
    core = row % 2
    partner = (row + 1 - 2 * core, col)
    across = ((row + 2 * core - 1 + TEAMS) % TEAMS, col)
    near = [device(1, 0), device(3, 0), device(0, 1), device(0, 3), partner, across]
    barrier = pltpu.get_barrier_semaphore()
    for one in near:
        pl.semaphore_signal(barrier, inc=1, device_id=one, device_id_type=MESH)
    ham_load = pltpu.make_async_copy(ham_in, ham, local_sems.at[0])
    inv_load = pltpu.make_async_copy(inv_in, inv_tiles, local_sems.at[1])
    ham_load.start()
    inv_load.start()
    bufs, signs = scratch[:SLOTS], scratch[SLOTS:]
    for ref in signs:
        ref[0] = jnp.zeros((BLOCK, OWN), BF16)
    for ref in bufs:
        ref[TEAM_BLOCKS] = jnp.zeros((BLOCK, OWN), BF16)
    own[TEAM_BLOCKS] = jnp.zeros((BLOCK, OWN), F32)
    onsites[4 * SLOTS] = jnp.zeros((1, OWN), F32)
    rolled[4 * SLOTS] = jnp.zeros((TILES, OWN, OWN), BF16)
    turned[SLOTS] = jnp.zeros((TILES, OWN_BLOCKS, BLOCK, OWN), BF16)
    lanes = lax.broadcasted_iota(jnp.int32, (OWN_BLOCKS, OWN), 1) // BLOCK
    spread = (lanes == lax.broadcasted_iota(jnp.int32, (OWN_BLOCKS, OWN), 0)).astype(F32)
    weights = lax.dot_general(
        pattern[...].astype(F32), spread, (((0,), (0,)), ((), ())), preferred_element_type=F32
    )
    ham_load.wait()
    for a in range(TEAM_BLOCKS):
        masked = ham[a * BLOCK : (a + 1) * BLOCK, :] * weights[a : a + 1, :]
        own[a] = masked
        bufs[0][a] = masked.astype(BF16)
    pl.semaphore_wait(barrier, len(near))

    def plane(region, rows, first):
        return Gather(region, rows, sems.at[0, pl.ds(first, 40)], sems.at[1, pl.ds(first, 40)], device)

    gather = plane(lambda oy, oz, start, size: bufs[oy * 4 + oz].at[pl.ds(start, size)], TEAM_BLOCKS, 0)
    gather.begin()
    for s in range(4):
        onsites[s * SLOTS : (s + 1) * SLOTS] = pltpu.roll(onsite[...], s * BLOCK, axis=1).reshape(SLOTS, 1, OWN)
    one_row = lax.broadcasted_iota(jnp.int32, (1, OWN), 1) // BLOCK

    def blocks(read, tile):
        return jnp.concatenate([read(listed[tile * 4 + q, group]) for q in range(4)], axis=0)

    @pl.loop(0, TILES)
    def _(tile):
        at = pl.ds(pl.multiple_of(tile * OWN, OWN), OWN)
        left[:, at] = blocks(lambda m: own[m], tile).T
        picked = jnp.zeros((1, OWN), F32)
        for q in range(4):
            line = onsites[onsite_at[tile * 4 + q, group]]
            picked = jnp.where(one_row == q, line, picked)
        diag[:, at] = picked

    def take_in(oy, oz):
        slot = oy * 4 + oz

        @pl.loop(0, TILES)
        def _(tile):
            x = blocks(lambda m: bufs[slot][m], tile)
            rolled[slot * 4, tile] = x
            x = x.astype(F32)
            turned[slot, tile] = x.T.astype(BF16).reshape(4, BLOCK, OWN)
            for s in (1, 2, 3):
                rolled[slot * 4 + s, tile] = pltpu.roll(x, s * BLOCK, axis=1).astype(BF16)

    take_in(0, 0)
    for n in FIRST:
        spot, whole = gather.arrive(n // 20, n % 20 // 4, n % 4)
        if whole:
            take_in(*spot)

    which = lax.broadcasted_iota(jnp.int32, (OWN, OWN), 1) // BLOCK
    eye = lax.broadcasted_iota(jnp.int32, (OWN, OWN), 0) == lax.broadcasted_iota(jnp.int32, (OWN, OWN), 1)

    def direct(up, over):
        tile = None
        for q in range(4):
            piece = rolled[rolled_at[over * 4 + q, group], up].astype(F32)
            tile = piece if tile is None else jnp.where(which == q, piece, tile)
        return tile

    def mirrored(up, over):
        pieces = []
        for q in range(4):
            a = up * 4 + q
            pieces.append(turned[slot_at[a, group], over, part_at[a, group]])
        return jnp.concatenate(pieces, axis=0).astype(F32)

    def assemble(n, total):
        up, over = n // TILES, n % TILES
        tile = 0.5 * (direct(up, over) + mirrored(up, over))
        mat[pl.ds(pl.multiple_of(up * OWN, OWN), OWN), pl.ds(pl.multiple_of(over * OWN, OWN), OWN)] = tile.astype(
            BF16
        )
        return total + jnp.sum((tile * tile).reshape(OWN // 8, 8, OWN), axis=0)

    total = lax.fori_loop(0, TILES * TILES, assemble, jnp.zeros((8, OWN), F32))

    extra = jnp.zeros((1, OWN), F32)
    start = []
    for tile in range(TILES):
        at = slice(tile * OWN, (tile + 1) * OWN)
        on_diag = jnp.sum(jnp.where(eye, mat[at, at].astype(F32), 0.0), axis=0, keepdims=True)
        energy = diag[:, at]
        extra += energy * (2.0 * on_diag + energy)
        first = 0.5 * (left[:, at] + direct(0, tile))
        if tile == 0:
            first += jnp.where(eye, energy, 0.0)
        start.append(first)
    count = (orders[group] * BLOCK).astype(F32)
    squares = jnp.sum(jnp.sum(total, axis=0, keepdims=True) + extra, axis=1, keepdims=True)
    scale = jnp.sqrt(count / (4.0 * (squares + 1e-06)))
    energy = diag[...]

    def apply(x, split=False):
        high = x.astype(BF16)
        if split:
            low = (x - high.astype(F32)).astype(BF16)
            y = jnp.dot(jnp.concatenate([high, low], axis=0), mat[...], preferred_element_type=F32)
            y = y[:OWN] + y[OWN:]
        else:
            y = jnp.dot(high, mat[...], preferred_element_type=F32)
        return scale * (y + x * energy)

    initial = scale * jnp.concatenate(start, axis=1)
    first_step = 1.5 * initial - 0.5 * apply(apply(initial))
    once = apply(first_step, split=True)
    once = 1.5 * once - 0.5 * apply(apply(once))
    twice = apply(once, split=True)
    twice = 1.5 * twice - 0.5 * apply(apply(twice))
    result = 1.5 * first_step - 0.5 * twice
    for tile in range(TILES):
        turned_back = result[:, tile * OWN : (tile + 1) * OWN].T.astype(BF16)
        signs[0][tile * 4 + 1 : tile * 4 + 5] = turned_back.reshape(4, BLOCK, OWN)
    gather.finish()
    inv_load.wait()

    def sign_at(team, oy, oz):
        return signs[team * SLOTS + oy * 4 + oz]

    def onward(team, oy, oz, start, size, n):
        return pltpu.make_async_remote_copy(
            src_ref=sign_at(0, oy, oz).at[pl.ds(start + 1, size)],
            dst_ref=sign_at(team, oy, oz).at[pl.ds(start + 1, size)],
            send_sem=sems.at[0, n],
            recv_sem=sems.at[1, n],
            device_id=partner if team == 1 else across,
            device_id_type=MESH,
        )

    def to_partner(oy, oz):
        return onward(1, oy, oz, 0, MEMBERS, 120 + oy * 4 + oz)

    def to_across(oy, oz, half):
        start = half * MEMBERS // 2 + SHARED // 2
        return onward(2, oy, oz, start, (MEMBERS - SHARED) // 2, 136 + half * SLOTS + oy * 4 + oz)

    shared = [onward(2, 0, 0, half * MEMBERS // 2, SHARED // 2, 168 + half) for half in (0, 1)]
    for half in (0, 1):
        shared[half].start()
    mine = plane(lambda oy, oz, start, size: sign_at(0, oy, oz).at[pl.ds(start + 1, size)], MEMBERS, 40)
    mine.begin()
    for half in (0, 1):
        to_across(0, 0, half).start()
    to_partner(0, 0).start()
    for half in (0, 1):
        shared[half].wait_recv()

    def shared_part(oy, oz, start, size):
        half = start // (SHARED // 2)
        return sign_at(2, oy, oz).at[pl.ds(half * MEMBERS // 2 + start % (SHARED // 2) + 1, size)]

    theirs = plane(shared_part, SHARED, 80)
    theirs.begin()

    sides = [1, 2 - 2 * core, 2 * core]
    teams = [row, partner[0], across[0]]

    def place(team, spot, t):
        slot = ((y + spot[0]) % 4) * 4 + (z + spot[1]) % 4
        line = teams[team] * SLOTS + slot

        @pl.loop(0, TEAM_BLOCKS // 16)
        def _(i):
            for j in range(16):
                b = i * 16 + j
                rows = pl.ds(pl.multiple_of(b * BLOCK, BLOCK), BLOCK)
                placed[rows, t * OWN : (t + 1) * OWN] = sign_at(team, *spot)[inverse[b, line]]

    def multiply(team, pair):
        side = sides[team]
        result = jnp.dot(inv_tiles[side], placed[...], preferred_element_type=F32)
        for t, (oy, oz) in enumerate(pair):
            slot = ((y + oy) % 4) * 4 + (z + oz) % 4
            out[side, :, pl.ds(pl.multiple_of(slot * OWN, OWN), OWN)] = result[:, t * OWN : (t + 1) * OWN]

    def work(team, pair):
        for t, spot in enumerate(pair):
            if team == 1:
                to_partner(*spot).wait_recv()
            if team == 2:
                to_across(*spot, 0).wait_recv()
                to_across(*spot, 1).wait_recv()
            place(team, spot, t)
            yield
        multiply(team, pair)
        yield

    order, order_theirs, todo = [(0, 0)], [(0, 0)], []
    for n in SECOND:
        half, ring, k = n % 40 // 20, n % 20 // 4, n % 4
        spot, whole = (mine if n < 40 else theirs).arrive(half, ring, k)
        if n < 40 and spot:
            to_across(*spot, half).start()
        if n < 40 and whole:
            order.append(spot)
            to_partner(*spot).start()
            if len(order) % 2 == 0:
                todo.append(work(0, order[-2:]))
                if len(order) > 2:
                    todo.append(work(1, order[-4:-2]))
            if len(order) == SLOTS:
                todo.append(work(1, order[-2:]))
        if n >= 40 and whole:
            order_theirs.append(spot)
            at = len(order_theirs) - LAG
            if at > 0 and at % 2 == 0:
                todo.append(work(2, order_theirs[at - 2 : at]))
        for _ in range(UNITS):
            while todo and next(todo[0], "end") == "end":
                todo.pop(0)
    for at in range(SLOTS - LAG, SLOTS, 2):
        todo.append(work(2, order_theirs[at : at + 2]))
    for steps in todo:
        for _ in steps:
            pass
    mine.finish()
    theirs.finish()
    for half in (0, 1):
        shared[half].wait_send()
        for one in order:
            to_across(*one, half).wait_send()
    for one in order:
        to_partner(*one).wait_send()


def shards(hamiltonian, pattern, onsite, members, orders, intersection_inv):
    smem = pl.BlockSpec(memory_space=pltpu.SMEM)
    vmem = pl.BlockSpec(memory_space=pltpu.VMEM)
    hbm = pl.BlockSpec(memory_space=pl.ANY)
    listed = members.T
    places_of = lax.broadcasted_iota(jnp.int32, (MEMBERS, TEAM_BLOCKS, TEAMS * SLOTS), 0) + 1
    hits = listed[:, None, :] == lax.broadcasted_iota(jnp.int32, places_of.shape, 1)
    inverse = jnp.sum(jnp.where(hits, places_of, 0), axis=0)
    col = lax.axis_index("col")
    at = lax.broadcasted_iota(jnp.int32, (MEMBERS, TEAMS * SLOTS), 0)
    part, block = listed & 3, listed >> 2
    slot = (((block >> 2) - (col >> 2)) & 3) * 4 + ((block - col) & 3)
    turn = (at - part) & 3
    active = at < orders
    tables = [
        jnp.where(active, values, idle)
        for values, idle in (
            (listed, TEAM_BLOCKS),
            (slot * 4 + turn, SLOTS * 4),
            (slot, SLOTS),
            (turn * SLOTS + block, SLOTS * 4),
            (part, 0),
        )
    ]
    density = pl.pallas_call(
        kernel,
        out_shape=pltpu.VMEM((3, OWN, TEAM_WIDTH), F32),
        in_specs=[smem] * 7 + [hbm, vmem, vmem, hbm],
        out_specs=vmem,
        scratch_shapes=[
            pltpu.VMEM((TEAM_WIDTH, OWN), F32),
            pltpu.VMEM((3, OWN, TEAM_WIDTH), BF16),
            pltpu.VMEM((TEAM_BLOCKS + 1, BLOCK, OWN), F32),
            pltpu.VMEM((4 * SLOTS + 1, 1, OWN), F32),
            pltpu.VMEM((OWN, SUB), F32),
            pltpu.VMEM((SLOTS * 4 + 1, TILES, OWN, OWN), BF16),
            pltpu.VMEM((SLOTS + 1, TILES, OWN_BLOCKS, BLOCK, OWN), BF16),
            pltpu.VMEM((SUB, SUB), BF16),
            pltpu.VMEM((1, SUB), F32),
            pltpu.VMEM((TEAM_WIDTH, 2 * OWN), BF16),
            pltpu.SemaphoreType.DMA((2,)),
            pltpu.SemaphoreType.DMA((2, 170)),
            *[pltpu.VMEM((TEAM_BLOCKS + 1, BLOCK, OWN), BF16) for _ in range(SLOTS)],
            *[pltpu.VMEM((MEMBERS + 1, BLOCK, OWN), BF16) for _ in range(3 * SLOTS)],
        ],
        compiler_params=pltpu.CompilerParams(
            collective_id=0, has_side_effects=True, vmem_limit_bytes=56 * 1024 * 1024
        ),
        name="density",
    )(
        *tables,
        orders,
        inverse,
        hamiltonian,
        pattern.T,
        onsite.reshape(SLOTS, OWN),
        intersection_inv.transpose(1, 0, 2),
    )
    return density.transpose(1, 0, 2)


def solution(mesh):
    in_specs = (P("row", "col"), P("row", "col"), P("row"), P(), P(), P(("row", "col"), None, None))
    out_specs = P(("row", "col"), None, None)
    return jax.shard_map(shards, mesh=mesh, in_specs=in_specs, out_specs=out_specs, check_vma=False)
```

```python
import jax
import jax.numpy as jnp
from jax import lax
from jax.experimental import pallas as pl
from jax.experimental.pallas import tpu as pltpu
from jax.sharding import PartitionSpec as P

BLOCK = 32
OWN_BLOCKS = 4
MEMBERS = 32
SLOTS = 16
TEAMS = 8
TEAM_BLOCKS = 64
TEAM_WIDTH = 2048
SUB = MEMBERS * BLOCK
OWN = OWN_BLOCKS * BLOCK
TILES = SUB // OWN
F32 = jnp.float32
BF16 = jnp.bfloat16
MESH = pl.DeviceIdType.MESH
SHARED = 12
LEAD = 10
LAG = 4
UNITS = 1
RINGS = ((0, 0), (0, 1), (1, 0), (1, 1), (0, 2), (0, 3), (4, 0), (4, 1), (2, 0), (2, 1))
RINGS += ((1, 2), (1, 3), (3, 0), (3, 1), (4, 2), (4, 3), (2, 2), (2, 3), (3, 2), (3, 3))
FIRST = [half * 20 + ring * 4 + k for ring, k in RINGS for half in (0, 1)]
SECOND = FIRST[:LEAD]
for lag in range(40 - LEAD):
    SECOND += [40 + FIRST[lag], FIRST[LEAD + lag]]
SECOND += [40 + n for n in FIRST[40 - LEAD :]]
RING_K = ((0, 3), (0, 1), (3, 2), (1, 2))


class Gather:
    def __init__(self, region, rows, send_sems, recv_sems, device):
        self.region, self.rows, self.device = region, rows, device
        self.send_sems, self.recv_sems = send_sems, recv_sems
        self.got, self.seen = {(0, 0): {0, 1}}, set()

    def copy(self, half, ring, k):
        source, landing = RING_K[k]
        step = 1 if k in (0, 2) else -1
        rows = self.rows // 2
        start, size = half * rows, rows
        if k >= 2:
            size = rows // 2
            start += size * (k - 2)

        def spot(offset):
            a, b = (offset, 0) if ring == 0 else (ring - 1, offset)
            return (b, a) if half == 0 else (a, b)

        along_z = (half == 0) == (ring == 0)
        n = half * 20 + ring * 4 + k
        return pltpu.make_async_remote_copy(
            src_ref=self.region(*spot(source), start, size),
            dst_ref=self.region(*spot(landing), start, size),
            send_sem=self.send_sems.at[n],
            recv_sem=self.recv_sems.at[n],
            device_id=self.device(0, step) if along_z else self.device(step, 0),
            device_id_type=MESH,
        ), spot(landing)

    def begin(self):
        for ring in (0, 1):
            for half in (0, 1):
                for k in (0, 1):
                    self.copy(half, ring, k)[0].start()

    def arrive(self, half, ring, k):
        copy, spot = self.copy(half, ring, k)
        copy.wait_recv()
        if k < 2:
            self.copy(half, ring, k + 2)[0].start()
        self.seen.add((half, ring, k))
        if k >= 2 and (half, ring, 5 - k) not in self.seen:
            return None, False
        if ring == 0:
            for j in (0, 1):
                self.copy(half, RING_K[k][1] + 1, j)[0].start()
        halves = self.got.setdefault(spot, set())
        halves.add(half)
        return spot, len(halves) == 2

    def finish(self):
        for half in (0, 1):
            for ring in range(5):
                for k in range(4):
                    self.copy(half, ring, k)[0].wait_send()


def places():
    row, col = lax.axis_index("row"), lax.axis_index("col")
    y, z = col // 4, col % 4

    def device(dy, dz):
        return (row, ((y + dy + 4) % 4) * 4 + (z + dz + 4) % 4)

    return row, col, y, z, device


def kernel(
    listed, rolled_at, slot_at, onsite_at, part_at, orders, inverse, ham_in, pattern, onsite, inv_in, out,
    ham, inv_tiles, own, onsites, left, rolled, turned, mat, diag, placed, local_sems, sems, *scratch
):
    row, col, y, z, device = places()
    group = row * SLOTS + col
    core = row % 2
    partner = (row + 1 - 2 * core, col)
    across = ((row + 2 * core - 1 + TEAMS) % TEAMS, col)
    near = [device(1, 0), device(3, 0), device(0, 1), device(0, 3), partner, across]
    barrier = pltpu.get_barrier_semaphore()
    for one in near:
        pl.semaphore_signal(barrier, inc=1, device_id=one, device_id_type=MESH)
    ham_load = pltpu.make_async_copy(ham_in, ham, local_sems.at[0])
    inv_load = pltpu.make_async_copy(inv_in, inv_tiles, local_sems.at[1])
    ham_load.start()
    inv_load.start()
    bufs, signs = scratch[:SLOTS], scratch[SLOTS:]
    for ref in signs:
        ref[0] = jnp.zeros((BLOCK, OWN), BF16)
    for ref in bufs:
        ref[TEAM_BLOCKS] = jnp.zeros((BLOCK, OWN), BF16)
    own[TEAM_BLOCKS] = jnp.zeros((BLOCK, OWN), F32)
    onsites[4 * SLOTS] = jnp.zeros((1, OWN), F32)
    rolled[4 * SLOTS] = jnp.zeros((TILES, OWN, OWN), BF16)
    turned[SLOTS] = jnp.zeros((TILES, OWN_BLOCKS, BLOCK, OWN), BF16)
    lanes = lax.broadcasted_iota(jnp.int32, (OWN_BLOCKS, OWN), 1) // BLOCK
    spread = (lanes == lax.broadcasted_iota(jnp.int32, (OWN_BLOCKS, OWN), 0)).astype(F32)
    weights = lax.dot_general(
        pattern[...].astype(F32), spread, (((0,), (0,)), ((), ())), preferred_element_type=F32
    )
    ham_load.wait()
    for a in range(TEAM_BLOCKS):
        masked = ham[a * BLOCK : (a + 1) * BLOCK, :] * weights[a : a + 1, :]
        own[a] = masked
        bufs[0][a] = masked.astype(BF16)
    pl.semaphore_wait(barrier, len(near))

    def plane(region, rows, first):
        return Gather(region, rows, sems.at[0, pl.ds(first, 40)], sems.at[1, pl.ds(first, 40)], device)

    gather = plane(lambda oy, oz, start, size: bufs[oy * 4 + oz].at[pl.ds(start, size)], TEAM_BLOCKS, 0)
    gather.begin()
    for s in range(4):
        onsites[s * SLOTS : (s + 1) * SLOTS] = pltpu.roll(onsite[...], s * BLOCK, axis=1).reshape(SLOTS, 1, OWN)
    one_row = lax.broadcasted_iota(jnp.int32, (1, OWN), 1) // BLOCK

    def blocks(read, tile):
        return jnp.concatenate([read(listed[tile * 4 + q, group]) for q in range(4)], axis=0)

    @pl.loop(0, TILES)
    def _(tile):
        at = pl.ds(pl.multiple_of(tile * OWN, OWN), OWN)
        left[:, at] = blocks(lambda m: own[m], tile).T
        picked = jnp.zeros((1, OWN), F32)
        for q in range(4):
            line = onsites[onsite_at[tile * 4 + q, group]]
            picked = jnp.where(one_row == q, line, picked)
        diag[:, at] = picked

    def take_in(oy, oz):
        slot = oy * 4 + oz

        @pl.loop(0, TILES)
        def _(tile):
            x = blocks(lambda m: bufs[slot][m], tile)
            rolled[slot * 4, tile] = x
            x = x.astype(F32)
            turned[slot, tile] = x.T.astype(BF16).reshape(4, BLOCK, OWN)
            for s in (1, 2, 3):
                rolled[slot * 4 + s, tile] = pltpu.roll(x, s * BLOCK, axis=1).astype(BF16)

    take_in(0, 0)
    for n in FIRST:
        spot, whole = gather.arrive(n // 20, n % 20 // 4, n % 4)
        if whole:
            take_in(*spot)

    which = lax.broadcasted_iota(jnp.int32, (OWN, OWN), 1) // BLOCK
    eye = lax.broadcasted_iota(jnp.int32, (OWN, OWN), 0) == lax.broadcasted_iota(jnp.int32, (OWN, OWN), 1)

    def direct(up, over):
        tile = None
        for q in range(4):
            piece = rolled[rolled_at[over * 4 + q, group], up].astype(F32)
            tile = piece if tile is None else jnp.where(which == q, piece, tile)
        return tile

    def mirrored(up, over):
        pieces = []
        for q in range(4):
            a = up * 4 + q
            pieces.append(turned[slot_at[a, group], over, part_at[a, group]])
        return jnp.concatenate(pieces, axis=0).astype(F32)

    def assemble(n, total):
        up, over = n // TILES, n % TILES
        tile = 0.5 * (direct(up, over) + mirrored(up, over))
        mat[pl.ds(pl.multiple_of(up * OWN, OWN), OWN), pl.ds(pl.multiple_of(over * OWN, OWN), OWN)] = tile.astype(
            BF16
        )
        return total + jnp.sum((tile * tile).reshape(OWN // 8, 8, OWN), axis=0)

    total = lax.fori_loop(0, TILES * TILES, assemble, jnp.zeros((8, OWN), F32), unroll=4)

    extra = jnp.zeros((1, OWN), F32)
    start = []
    for tile in range(TILES):
        at = slice(tile * OWN, (tile + 1) * OWN)
        on_diag = jnp.sum(jnp.where(eye, mat[at, at].astype(F32), 0.0), axis=0, keepdims=True)
        energy = diag[:, at]
        extra += energy * (2.0 * on_diag + energy)
        first = 0.5 * (left[:, at] + direct(0, tile))
        if tile == 0:
            first += jnp.where(eye, energy, 0.0)
        start.append(first)
    count = (orders[group] * BLOCK).astype(F32)
    squares = jnp.sum(jnp.sum(total, axis=0, keepdims=True) + extra, axis=1, keepdims=True)
    scale = jnp.sqrt(count / (4.0 * (squares + 1e-06)))
    energy = diag[...]

    def apply(x, split=False):
        high = x.astype(BF16)
        if split:
            low = (x - high.astype(F32)).astype(BF16)
            y = jnp.dot(jnp.concatenate([high, low], axis=0), mat[...], preferred_element_type=F32)
            y = y[:OWN] + y[OWN:]
        else:
            y = jnp.dot(high, mat[...], preferred_element_type=F32)
        return scale * (y + x * energy)

    initial = scale * jnp.concatenate(start, axis=1)
    first_step = 1.5 * initial - 0.5 * apply(apply(initial))
    once = apply(first_step, split=True)
    once = 1.5 * once - 0.5 * apply(apply(once))
    twice = apply(once, split=True)
    twice = 1.5 * twice - 0.5 * apply(apply(twice))
    result = 1.5 * first_step - 0.5 * twice
    for tile in range(TILES):
        turned_back = result[:, tile * OWN : (tile + 1) * OWN].T.astype(BF16)
        signs[0][tile * 4 + 1 : tile * 4 + 5] = turned_back.reshape(4, BLOCK, OWN)
    gather.finish()
    inv_load.wait()

    def sign_at(team, oy, oz):
        return signs[team * SLOTS + oy * 4 + oz]

    def onward(team, oy, oz, start, size, n):
        return pltpu.make_async_remote_copy(
            src_ref=sign_at(0, oy, oz).at[pl.ds(start + 1, size)],
            dst_ref=sign_at(team, oy, oz).at[pl.ds(start + 1, size)],
            send_sem=sems.at[0, n],
            recv_sem=sems.at[1, n],
            device_id=partner if team == 1 else across,
            device_id_type=MESH,
        )

    def to_partner(oy, oz):
        return onward(1, oy, oz, 0, MEMBERS, 120 + oy * 4 + oz)

    def to_across(oy, oz, half):
        start = half * MEMBERS // 2 + SHARED // 2
        return onward(2, oy, oz, start, (MEMBERS - SHARED) // 2, 136 + half * SLOTS + oy * 4 + oz)

    shared = [onward(2, 0, 0, half * MEMBERS // 2, SHARED // 2, 168 + half) for half in (0, 1)]
    for half in (0, 1):
        shared[half].start()
    mine = plane(lambda oy, oz, start, size: sign_at(0, oy, oz).at[pl.ds(start + 1, size)], MEMBERS, 40)
    mine.begin()
    for half in (0, 1):
        to_across(0, 0, half).start()
    to_partner(0, 0).start()
    for half in (0, 1):
        shared[half].wait_recv()

    def shared_part(oy, oz, start, size):
        half = start // (SHARED // 2)
        return sign_at(2, oy, oz).at[pl.ds(half * MEMBERS // 2 + start % (SHARED // 2) + 1, size)]

    theirs = plane(shared_part, SHARED, 80)
    theirs.begin()

    sides = [1, 2 - 2 * core, 2 * core]
    teams = [row, partner[0], across[0]]

    def place(team, spot, t):
        slot = ((y + spot[0]) % 4) * 4 + (z + spot[1]) % 4
        line = teams[team] * SLOTS + slot

        @pl.loop(0, TEAM_BLOCKS // 16)
        def _(i):
            for j in range(16):
                b = i * 16 + j
                rows = pl.ds(pl.multiple_of(b * BLOCK, BLOCK), BLOCK)
                placed[rows, t * OWN : (t + 1) * OWN] = sign_at(team, *spot)[inverse[b, line]]

    def multiply(team, pair):
        side = sides[team]
        result = jnp.dot(inv_tiles[side], placed[...], preferred_element_type=F32)
        for t, (oy, oz) in enumerate(pair):
            slot = ((y + oy) % 4) * 4 + (z + oz) % 4
            out[side, :, pl.ds(pl.multiple_of(slot * OWN, OWN), OWN)] = result[:, t * OWN : (t + 1) * OWN]

    def work(team, pair):
        for t, spot in enumerate(pair):
            if team == 1:
                to_partner(*spot).wait_recv()
            if team == 2:
                to_across(*spot, 0).wait_recv()
                to_across(*spot, 1).wait_recv()
            place(team, spot, t)
            yield
        multiply(team, pair)
        yield

    order, order_theirs, todo = [(0, 0)], [(0, 0)], []
    for n in SECOND:
        half, ring, k = n % 40 // 20, n % 20 // 4, n % 4
        spot, whole = (mine if n < 40 else theirs).arrive(half, ring, k)
        if n < 40 and spot:
            to_across(*spot, half).start()
        if n < 40 and whole:
            order.append(spot)
            to_partner(*spot).start()
            if len(order) % 2 == 0:
                todo.append(work(0, order[-2:]))
                if len(order) > 2:
                    todo.append(work(1, order[-4:-2]))
            if len(order) == SLOTS:
                todo.append(work(1, order[-2:]))
        if n >= 40 and whole:
            order_theirs.append(spot)
            at = len(order_theirs) - LAG
            if at > 0 and at % 2 == 0:
                todo.append(work(2, order_theirs[at - 2 : at]))
        for _ in range(UNITS):
            while todo and next(todo[0], "end") == "end":
                todo.pop(0)
    for at in range(SLOTS - LAG, SLOTS, 2):
        todo.append(work(2, order_theirs[at : at + 2]))
    for steps in todo:
        for _ in steps:
            pass
    mine.finish()
    theirs.finish()
    for half in (0, 1):
        shared[half].wait_send()
        for one in order:
            to_across(*one, half).wait_send()
    for one in order:
        to_partner(*one).wait_send()


def shards(hamiltonian, pattern, onsite, members, orders, intersection_inv):
    smem = pl.BlockSpec(memory_space=pltpu.SMEM)
    vmem = pl.BlockSpec(memory_space=pltpu.VMEM)
    hbm = pl.BlockSpec(memory_space=pl.ANY)
    listed = members.T
    places_of = lax.broadcasted_iota(jnp.int32, (MEMBERS, TEAM_BLOCKS, TEAMS * SLOTS), 0) + 1
    hits = listed[:, None, :] == lax.broadcasted_iota(jnp.int32, places_of.shape, 1)
    inverse = jnp.sum(jnp.where(hits, places_of, 0), axis=0)
    col = lax.axis_index("col")
    at = lax.broadcasted_iota(jnp.int32, (MEMBERS, TEAMS * SLOTS), 0)
    part, block = listed & 3, listed >> 2
    slot = (((block >> 2) - (col >> 2)) & 3) * 4 + ((block - col) & 3)
    turn = (at - part) & 3
    active = at < orders
    tables = [
        jnp.where(active, values, idle)
        for values, idle in (
            (listed, TEAM_BLOCKS),
            (slot * 4 + turn, SLOTS * 4),
            (slot, SLOTS),
            (turn * SLOTS + block, SLOTS * 4),
            (part, 0),
        )
    ]
    density = pl.pallas_call(
        kernel,
        out_shape=pltpu.VMEM((3, OWN, TEAM_WIDTH), F32),
        in_specs=[smem] * 7 + [hbm, vmem, vmem, hbm],
        out_specs=vmem,
        scratch_shapes=[
            pltpu.VMEM((TEAM_WIDTH, OWN), F32),
            pltpu.VMEM((3, OWN, TEAM_WIDTH), BF16),
            pltpu.VMEM((TEAM_BLOCKS + 1, BLOCK, OWN), F32),
            pltpu.VMEM((4 * SLOTS + 1, 1, OWN), F32),
            pltpu.VMEM((OWN, SUB), F32),
            pltpu.VMEM((SLOTS * 4 + 1, TILES, OWN, OWN), BF16),
            pltpu.VMEM((SLOTS + 1, TILES, OWN_BLOCKS, BLOCK, OWN), BF16),
            pltpu.VMEM((SUB, SUB), BF16),
            pltpu.VMEM((1, SUB), F32),
            pltpu.VMEM((TEAM_WIDTH, 2 * OWN), BF16),
            pltpu.SemaphoreType.DMA((2,)),
            pltpu.SemaphoreType.DMA((2, 170)),
            *[pltpu.VMEM((TEAM_BLOCKS + 1, BLOCK, OWN), BF16) for _ in range(SLOTS)],
            *[pltpu.VMEM((MEMBERS + 1, BLOCK, OWN), BF16) for _ in range(3 * SLOTS)],
        ],
        compiler_params=pltpu.CompilerParams(
            collective_id=0, has_side_effects=True, vmem_limit_bytes=56 * 1024 * 1024
        ),
        name="density",
    )(
        *tables,
        orders,
        inverse,
        hamiltonian,
        pattern.T,
        onsite.reshape(SLOTS, OWN),
        intersection_inv.transpose(1, 0, 2),
    )
    return density.transpose(1, 0, 2)


def solution(mesh):
    in_specs = (P("row", "col"), P("row", "col"), P("row"), P(), P(), P(("row", "col"), None, None))
    out_specs = P(("row", "col"), None, None)
    return jax.shard_map(shards, mesh=mesh, in_specs=in_specs, out_specs=out_specs, check_vma=False)
```
